32 devices in a mesh: dp: 2 (over core), ctx: 4 (over z), tensor: 4 (over y, x).
Axes of the slice: x: 2, y: 2, z: 4, core: 2. Of those that a mesh axis runs over, the one named last changes fastest.
Arguments:
- tokens: bfloat16 [4096, 2048], P(('dp', 'ctx')), may hold values from -6 to 6
- lengths: int32 [2, 13], P('dp'), may hold values from 1 to 819, 2048 in all within a row
- parents: int32 [2, 13], P('dp'), may hold values from 0 to 4, as said below
- w_query: bfloat16 [2048, 2048], P(('dp', 'ctx'), 'tensor'), may hold values from -0.125 to 0.125
- w_key: bfloat16 [2048, 1024], P(('dp', 'ctx'), 'tensor'), may hold values from -0.125 to 0.125
- w_value: bfloat16 [2048, 1024], P(('dp', 'ctx'), 'tensor'), may hold values from -0.125 to 0.125
- w_out: bfloat16 [2048, 2048], P('tensor', ('dp', 'ctx')), may hold values from -1.5 to 1.5
- w_gate: bfloat16 [2048, 6144], P(('dp', 'ctx'), 'tensor'), may hold values from -0.125 to 0.125
- w_up: bfloat16 [2048, 6144], P(('dp', 'ctx'), 'tensor'), may hold values from -0.125 to 0.125
- w_down: bfloat16 [6144, 2048], P('tensor', ('dp', 'ctx')), may hold values from -0.078125 to 0.078125
- gain_attn: bfloat16 [2048], P(('dp', 'ctx')), may hold values from 0.099609375 to 1.8984375
- gain_mlp: bfloat16 [2048], P(('dp', 'ctx')), may hold values from 0.099609375 to 1.8984375
- gain_query: bfloat16 [128], P(('dp', 'ctx')), may hold values from 0.099609375 to 1.8984375
- gain_key: bfloat16 [128], P(('dp', 'ctx')), may hold values from 0.099609375 to 1.8984375
- cotangent: bfloat16 [4096, 2048], P(('dp', 'ctx')), may hold values from -6 to 6
Outputs:
- result: bfloat16 [4096, 2048], P(('dp', 'ctx'))
- grad_tokens: float32 [4096, 2048], P(('dp', 'ctx'))
- grad_query: float32 [2048, 2048], P(('dp', 'ctx'), 'tensor')
- grad_key: float32 [2048, 1024], P(('dp', 'ctx'), 'tensor')
- grad_value: float32 [2048, 1024], P(('dp', 'ctx'), 'tensor')
- grad_out: float32 [2048, 2048], P('tensor', ('dp', 'ctx'))
- grad_gate: float32 [2048, 6144], P(('dp', 'ctx'), 'tensor')
- grad_up: float32 [2048, 6144], P(('dp', 'ctx'), 'tensor')
- grad_down: float32 [6144, 2048], P('tensor', ('dp', 'ctx'))
- grad_gain_attn: float32 [2048], P(('dp', 'ctx'))
- grad_gain_mlp: float32 [2048], P(('dp', 'ctx'))
- grad_gain_query: float32 [128], P(('dp', 'ctx'))
- grad_gain_key: float32 [128], P(('dp', 'ctx'))
The draws below stay inside these ranges and needn't reach their ends.
Inputs may be any that keep to these rules, and one draw needn't show every extreme that they name: lengths[t, s] counts the tokens of segment s of tree t; the segments lie in order and each tree's lengths sum to 2048. parents[t, s] is the segment from which segment s of tree t hangs; segments 0 to 4 name 0 (segment 0 is the root), segments 5 to 12 name one of 1 to 4.
All inputs are finite; a program needn't handle non-finite values.
Results may differ from the reference program's by a relative error of at most 0.02.
Values may be sent and summed in bfloat16 or wider, within the bound.
No kernel may reach another device: no remote copies, remote signals or barrier semaphores. Data moves between devices by JAX's collectives and lax.ppermute only.
A program may use at most 192 MiB of HBM per device.

```python
import math
import jax
import jax.numpy as jnp
import numpy as np
from jax import lax

D = 2048
FF = 6144
HEADS = 16
KV_HEADS = 8
HEAD_DIM = 128
SEGS = 13
TREE_LEN = 2048
TREES = 2
TOKENS = 4096
MOST = 819


def draw_parents(key, part):
    leaf_count = SEGS - 5
    leaf_parents = jax.random.randint(key, (TREES, leaf_count), 1, 5).astype(jnp.int32)
    first_leaf = jnp.ones((TREES, 1), jnp.int32)
    last_leaf = jnp.full((TREES, 1), 4, jnp.int32)
    upper_part = jnp.zeros((TREES, 5), jnp.int32)
    return jnp.concatenate([upper_part, first_leaf, leaf_parents[:, 1:-1], last_leaf], axis=1)


def strengthened(entries, key, source, target, parts, factor):
    def block_of(dim):
        return (jnp.arange(entries.shape[dim]) // (entries.shape[dim] // parts)).reshape((-1,) + (1,) * (entries.ndim - 1 - dim))

    one_side = jax.random.permutation(key, parts)[block_of(target)]
    other_side = (block_of(target) + parts // 2) % parts
    return jnp.where((block_of(source) == one_side) | (block_of(source) == other_side), factor * entries, entries)


def steps_of(key, dims, cuts, least, largest):
    def one(axis_at, blocks):
        heights = jax.random.uniform(jax.random.fold_in(jax.random.fold_in(key, 6), axis_at), (blocks,), jnp.float32, least / len(cuts), largest / len(cuts))
        return jnp.repeat(jnp.exp(heights), dims[axis_at] // blocks).reshape((-1,) + (1,) * (len(dims) - axis_at - 1))

    level = one(*cuts[0])
    for cut in cuts[1:]:
        level = level * one(*cut)
    return level


def profile(count, total, most, skew):
    weights = [(1 << 20) // math.isqrt(rank ** skew) + 1 for rank in range(2, count + 1)]
    surplus, holding = total - most - (count - 1), [1] * (count - 1)
    while surplus > 0:
        candidates = [i for i in range(count - 1) if holding[i] < most]
        whole, remaining = sum([weights[i] for i in candidates]), surplus
        for i in candidates:
            more = min(most - holding[i], max(1, remaining * weights[i] // whole), surplus)
            holding[i] = holding[i] + more
            surplus = surplus - more
    return np.array([most] + holding)


def uneven(own_key, amount, total, most, slope):
    if amount == 2:
        one = jax.random.randint(own_key, (), max(1, total - most), min(most, total - 1) + 1)
        return jnp.stack([one, total - one])
    tallies = jnp.asarray(profile(amount, total, most, slope), jnp.int32)
    pairs = (amount - 1) // 2
    giver, taker = tallies[1:1 + 2 * pairs:2], tallies[2:2 + 2 * pairs:2]
    margin = jnp.minimum(giver - 1, most - taker)
    passed = jax.random.randint(jax.random.fold_in(own_key, 1), (pairs,), 0, 1 << 20) % (margin + 1)
    tallies = tallies.at[1:1 + 2 * pairs:2].set(giver - passed).at[2:2 + 2 * pairs:2].set(taker + passed)
    return tallies[jax.random.permutation(jax.random.fold_in(own_key, 2), amount)]


def bell_draw(rng, extent, deviation, most, cuts=(), kind=jnp.bfloat16):
    level = steps_of(rng, extent, cuts, -0.22, 0.18) if cuts else 1.0
    values = jax.random.normal(rng, extent, jnp.float32) * deviation * level
    return jnp.minimum(jnp.maximum(values, -most), most).astype(kind)


def bell_draw_with(rng, shape, width, bound, cuts, heavy, kind=jnp.bfloat16):
    drawn = width * jax.random.normal(rng, shape, jnp.float32)
    if cuts:
        drawn = drawn * steps_of(rng, shape, cuts, -0.22, 0.18)
    return jnp.clip(strengthened(drawn, jax.random.fold_in(rng, 3), *heavy), -bound, bound).astype(kind)


def setup_inputs(seed: int = 0) -> dict:
    key_of = jax.random.split(jax.random.key(seed), 16)
    tokens = bell_draw(key_of[0], (TOKENS, D), 1.0, 6.0, ((0, 8),))
    lengths = jax.vmap(lambda own: uneven(own, SEGS, TREE_LEN, MOST, 1))(jax.random.split(key_of[1], TREES)).reshape((TREES, SEGS)).astype(jnp.int32)
    parents = draw_parents(jax.random.fold_in(key_of[15], 71), 0)
    w_query = bell_draw(key_of[3], (D, HEADS * HEAD_DIM), D ** -0.5, 0.125, ((0, 8), (1, 4)))
    w_key = bell_draw(key_of[4], (D, KV_HEADS * HEAD_DIM), D ** -0.5, 0.125, ((0, 8), (1, 4)))
    w_value = bell_draw(key_of[5], (D, KV_HEADS * HEAD_DIM), D ** -0.5, 0.125, ((0, 8), (1, 4)))
    w_out = bell_draw(key_of[6], (HEADS * HEAD_DIM, D), (HEADS * HEAD_DIM // 128) ** -0.5, 1.5, ((0, 4), (1, 8)))
    w_gate = bell_draw(key_of[7], (D, FF), D ** -0.5, 0.125, ((0, 8), (1, 4)))
    w_up = bell_draw(key_of[8], (D, FF), D ** -0.5, 0.125, ((0, 8), (1, 4)))
    w_down = bell_draw(key_of[9], (FF, D), FF ** -0.5, 0.078125, ((0, 4), (1, 8)))
    gain_attn = jnp.clip(1.0 + 0.18 * jax.random.normal(key_of[10], (D,), jnp.float32), 0.099609375, 1.8984375).astype(jnp.bfloat16)
    gain_mlp = jnp.clip(1.0 + 0.18 * jax.random.normal(key_of[11], (D,), jnp.float32), 0.099609375, 1.8984375).astype(jnp.bfloat16)
    gain_query = jnp.clip(1.0 + 0.18 * jax.random.normal(key_of[12], (HEAD_DIM,), jnp.float32), 0.099609375, 1.8984375).astype(jnp.bfloat16)
    gain_key = jnp.clip(1.0 + 0.18 * jax.random.normal(key_of[13], (HEAD_DIM,), jnp.float32), 0.099609375, 1.8984375).astype(jnp.bfloat16)
    cotangent = bell_draw_with(key_of[14], (TOKENS, D), 1.0, 6.0, ((0, 8),), (0, 1, 8, 2.0))
    return dict(tokens=tokens, lengths=lengths, parents=parents, w_query=w_query, w_key=w_key, w_value=w_value, w_out=w_out, w_gate=w_gate, w_up=w_up, w_down=w_down, gain_attn=gain_attn, gain_mlp=gain_mlp, gain_query=gain_query, gain_key=gain_key, cotangent=cotangent)


@jax.custom_vjp
def low(v):
    return lax.optimization_barrier(v.astype(jnp.bfloat16)).astype(jnp.float32)

@jax.custom_vjp
def low_back(v):
    return v

def low_keep(v):
    return (low(v), None)

def low_pass(kept, grad):
    return (grad,)

def back_keep(v):
    return (v, None)

def back_low(kept, grad):
    return (low(grad),)
low.defvjp(low_keep, low_pass)
low_back.defvjp(back_keep, back_low)
EPS = 1e-06
THETA = 1000000.0
PRECISE = lax.Precision.HIGHEST

def rounded_both(values):
    return low(low_back(values))

def matmul(left, right):
    return jnp.dot(left, right, precision=PRECISE)

def norm_rows(values, gain_vec):
    return values * lax.rsqrt(lax.optimization_barrier(jnp.mean(values * values, axis=-1, keepdims=True)) + EPS) * gain_vec

def rotate_pairs(values, cosine, sine_vals):
    half_dim = values.shape[-1] // 2
    first_half = values[..., :half_dim]
    second_half = values[..., half_dim:]
    return jnp.concatenate([first_half * cosine - second_half * sine_vals, second_half * cosine + first_half * sine_vals], axis=-1)

def tree_layout(lengths, parents, tree_total):
    seg_count = lengths.shape[0]
    index = jnp.arange(seg_count, dtype=jnp.int32)
    direct = ((parents[:, None] == index[None, :]) & (parents[:, None] != index[:, None])).astype(jnp.float32)
    reach = direct
    for closure_step in range(4):
        reach = jnp.minimum(reach + jnp.dot(reach, reach, precision=PRECISE), 1.0)
    ends = jnp.cumsum(lengths, dtype=jnp.int32)
    starts = (ends - lengths).astype(jnp.int32)
    offset = jnp.dot(reach, lengths.astype(jnp.float32), precision=PRECISE)
    places = jnp.arange(tree_total, dtype=jnp.int32)
    member = (starts[None, :] <= places[:, None]).astype(jnp.int32)
    segment_ids = (lax.optimization_barrier(jnp.sum(member, axis=1, dtype=jnp.int32)) - 1).astype(jnp.int32)
    onehot = (segment_ids[:, None] == index[None, :]).astype(jnp.float32)
    base = jnp.dot(onehot, offset - starts.astype(jnp.float32), precision=PRECISE)
    position = places.astype(jnp.float32) + base
    return (segment_ids, onehot, reach, position)

def tree_forward(inputs, lengths, parents, w_query, w_key, w_value, w_out, w_gate, w_up, w_down, gain_attn, gain_mlp, gain_query, gain_key):
    tree_total = inputs.shape[0]
    segment_ids, onehot, reach, position = tree_layout(lengths, parents, tree_total)
    places = jnp.arange(tree_total, dtype=jnp.int32)
    ancestor = matmul(matmul(onehot, reach), onehot.T) > 0.5
    allowed = (segment_ids[:, None] == segment_ids[None, :]) & (places[None, :] <= places[:, None]) | ancestor
    half_dim = HEAD_DIM // 2
    frequency = jnp.exp(jnp.arange(half_dim, dtype=jnp.float32) * (-2.0 * math.log(THETA) / HEAD_DIM))
    angles = position[:, None] * frequency[None, :]
    cosine = jnp.cos(angles)[:, None, :]
    sine_vals = jnp.sin(angles)[:, None, :]
    group_size = HEADS // KV_HEADS
    normed_attn = low(norm_rows(inputs, gain_attn))
    queries = low_back(matmul(normed_attn, w_query)).reshape(tree_total, HEADS, HEAD_DIM)
    key_vecs = low_back(matmul(normed_attn, w_key)).reshape(tree_total, KV_HEADS, HEAD_DIM)
    values = rounded_both(matmul(normed_attn, w_value)).reshape(tree_total, KV_HEADS, HEAD_DIM)
    queries = rounded_both(rotate_pairs(norm_rows(queries, gain_query), cosine, sine_vals))
    key_vecs = rounded_both(rotate_pairs(norm_rows(key_vecs, gain_key), cosine, sine_vals))
    score_scale = 1.0 / math.sqrt(HEAD_DIM)
    grouped = queries.reshape(tree_total, KV_HEADS, group_size, HEAD_DIM).transpose(1, 2, 0, 3)

    def attend(pieces):
        q_part, k_part, v_part = pieces
        scores = low_back(jnp.einsum('gqd,kd->gqk', q_part, k_part, precision=PRECISE) * score_scale)
        scores = jnp.where(allowed[None], scores, -1e+30)
        row_max = lax.optimization_barrier(jnp.max(scores, axis=-1, keepdims=True))
        weights = jnp.exp(scores - row_max)
        prob_all = weights / lax.optimization_barrier(jnp.sum(weights, axis=-1, keepdims=True))
        return jnp.einsum('gqk,kd->gqd', low(prob_all), v_part, precision=PRECISE)
    mixture = lax.map(jax.checkpoint(attend), (grouped, key_vecs.transpose(1, 0, 2), values.transpose(1, 0, 2)))
    mixture = rounded_both(mixture.transpose(2, 0, 1, 3).reshape(tree_total, HEADS * HEAD_DIM))
    hidden = inputs + low_back(matmul(mixture, w_out))
    normed_mlp = low(norm_rows(hidden, gain_mlp))
    gate_pre = low_back(matmul(normed_mlp, w_gate))
    up_pre = low_back(matmul(normed_mlp, w_up))
    inner_act = low(gate_pre * jax.nn.sigmoid(gate_pre) * up_pre)
    return hidden + low_back(matmul(inner_act, w_down))

def reference(tokens, lengths, parents, w_query, w_key, w_value, w_out, w_gate, w_up, w_down, gain_attn, gain_mlp, gain_query, gain_key, cotangent):
    params = tuple((item.astype(jnp.float32) for item in (w_query, w_key, w_value, w_out, w_gate, w_up, w_down, gain_attn, gain_mlp, gain_query, gain_key)))
    inputs = tokens.astype(jnp.float32)

    def forward(layer_in, *layer_params):
        tree_rows = layer_in.reshape(TREES, TREE_LEN, D)

        def per_tree(pieces):
            tree_in, tree_lengths, tree_parents = pieces
            return tree_forward(tree_in, tree_lengths, tree_parents, *layer_params)
        outputs = lax.map(jax.checkpoint(per_tree), (tree_rows, lengths, parents))
        return outputs.reshape(TREES * TREE_LEN, D)
    result, pullback = jax.vjp(forward, inputs, *params)
    gradients = pullback(cotangent.astype(jnp.float32))
    return (result.astype(jnp.bfloat16), gradients[0], gradients[1], gradients[2], gradients[3], gradients[4], gradients[5], gradients[6], gradients[7], gradients[8], gradients[9], gradients[10], gradients[11])
```

```python
import math

import jax
import jax.numpy as jnp
from jax import lax
from jax.sharding import PartitionSpec as P

HEAD_DIM = 128

EPS = 1e-06
THETA = 1000000.0
PRECISE = lax.Precision.HIGHEST
BF = jnp.bfloat16
F32 = jnp.float32
ROWS = ("dp", "ctx")


def row_scales(values):
    return lax.rsqrt(jnp.mean(values * values, axis=-1, keepdims=True) + EPS)


def norm_back(grad_in, values, gain_vec, scales):
    upstream = grad_in * gain_vec
    inner_mean = jnp.mean(upstream * values, axis=-1, keepdims=True)
    return (
        scales * upstream - values * scales * scales * scales * inner_mean,
        grad_in * values * scales,
    )


def rotate_pairs(values, cosine, sine_vals):
    half_dim = values.shape[-1] // 2
    first_half = values[..., :half_dim]
    second_half = values[..., half_dim:]
    return jnp.concatenate(
        [
            first_half * cosine - second_half * sine_vals,
            second_half * cosine + first_half * sine_vals,
        ],
        axis=-1,
    )


def rotate_back(values, cosine, sine_vals):
    return rotate_pairs(values, cosine, -sine_vals)


def dot(left, right):
    return jnp.dot(left, right, preferred_element_type=F32)


def inner_rows(left, right):
    return lax.dot_general(left, right, (((0,), (0,)), ((), ())), preferred_element_type=F32)


def outer_cols(left, right):
    return lax.dot_general(left, right, (((1,), (1,)), ((), ())), preferred_element_type=F32)


def swap(values, axis, mask):
    size = lax.axis_size(axis)
    return lax.ppermute(values, axis, [(a, a ^ mask) for a in range(size)])


def scatter_sum(partial):
    size = lax.axis_size("tensor")
    chunk = partial.shape[0] // size
    low = partial.astype(BF)
    total = partial[:chunk]
    for mask in range(1, size):
        total = total + swap(low[mask * chunk : (mask + 1) * chunk], "tensor", mask).astype(F32)
    return total


def gather_rows(own):
    size = lax.axis_size("tensor")
    return [own] + [swap(own, "tensor", mask) for mask in range(1, size)]


def xor_order(values):
    size = lax.axis_size("tensor")
    me = lax.axis_index("tensor")
    chunk = values.shape[0] // size
    return jnp.concatenate(
        [
            lax.dynamic_slice_in_dim(values, (me ^ mask) * chunk, chunk, axis=0)
            for mask in range(size)
        ],
        axis=0,
    )


def grad_scatter(left, right):
    half = left.shape[1] // 2
    me = lax.axis_index("dp")
    theirs = lax.dynamic_slice_in_dim(left, (1 - me) * half, half, axis=1)
    mine = lax.dynamic_slice_in_dim(left, me * half, half, axis=1)
    sent = swap(inner_rows(theirs, right).astype(BF), "dp", 1)
    both = (inner_rows(mine, right) + sent.astype(F32)).astype(BF)
    return lax.psum_scatter(both, "ctx", scatter_dimension=0, tiled=True)


def tree_layout(lengths, parents, tree_total):
    seg_count = lengths.shape[0]
    index = jnp.arange(seg_count, dtype=jnp.int32)
    direct = ((parents[:, None] == index[None, :]) & (parents[:, None] != index[:, None])).astype(
        F32
    )
    reach = direct
    for closure_step in range(4):
        reach = jnp.minimum(reach + jnp.dot(reach, reach, precision=PRECISE), 1.0)
    ends = jnp.cumsum(lengths, dtype=jnp.int32)
    starts = ends - lengths
    offset = jnp.dot(reach, lengths.astype(F32), precision=PRECISE)
    return starts, reach, offset


def segment_onehot(places, starts):
    index = jnp.arange(starts.shape[0], dtype=jnp.int32)
    member = (starts[None, :] <= places[:, None]).astype(jnp.int32)
    segment_ids = jnp.sum(member, axis=1, dtype=jnp.int32) - 1
    return segment_ids, (segment_ids[:, None] == index[None, :]).astype(F32)


def on_device(
    tokens,
    lengths,
    parents,
    w_query,
    w_key,
    w_value,
    w_out,
    w_gate,
    w_up,
    w_down,
    gain_attn,
    gain_mlp,
    gain_query,
    gain_key,
    cotangent,
):
    row_count, width = tokens.shape
    ctx_size = lax.axis_size("ctx")
    split = lax.axis_size("tensor")
    me_t = lax.axis_index("tensor")
    chunk = row_count // split
    tree_total = row_count * ctx_size
    q_cols, k_cols = w_query.shape[1], w_key.shape[1]

    w_qkv = lax.all_gather(
        jnp.concatenate([w_query, w_key, w_value], axis=1), ROWS, axis=0, tiled=True
    )
    wo_t = lax.all_gather(w_out.T, ROWS, axis=0, tiled=True)
    wg_full = lax.all_gather(w_gate, ROWS, axis=0, tiled=True)
    wu_full = lax.all_gather(w_up, ROWS, axis=0, tiled=True)
    wd_t = lax.all_gather(w_down.T, ROWS, axis=0, tiled=True)

    gain_sizes = (gain_attn.shape[0], gain_mlp.shape[0], gain_query.shape[0], gain_key.shape[0])
    gains = lax.all_gather(
        jnp.concatenate([gain_attn, gain_mlp, gain_query, gain_key])[None], ROWS, axis=0, tiled=True
    ).astype(F32)
    gain_parts, place = [], 0
    for size in gain_sizes:
        gain_parts.append(gains[:, place : place + size].reshape(-1))
        place += size
    gain_one, gain_two, gain_q, gain_k = gain_parts

    local = jnp.arange(row_count, dtype=jnp.int32)
    natural = ((local // chunk) ^ me_t) * chunk + local % chunk
    place_here = lax.axis_index("ctx") * row_count + natural
    place_all = (
        jnp.arange(ctx_size, dtype=jnp.int32)[:, None] * row_count + natural[None, :]
    ).reshape(-1)
    starts, reach, offset = tree_layout(lengths[0], parents[0], tree_total)
    segment_here, onehot_here = segment_onehot(place_here, starts)
    segment_all, onehot_all = segment_onehot(place_all, starts)
    position = place_here.astype(F32) + jnp.dot(
        onehot_here, offset - starts.astype(F32), precision=PRECISE
    )
    ancestor = (
        jnp.dot(jnp.dot(onehot_here, reach, precision=PRECISE), onehot_all.T, precision=PRECISE)
        > 0.5
    )
    allowed = (segment_here[:, None] == segment_all[None, :]) & (
        place_all[None, :] <= place_here[:, None]
    ) | ancestor
    half_dim = HEAD_DIM // 2
    frequency = jnp.exp(jnp.arange(half_dim, dtype=F32) * (-2.0 * math.log(THETA) / HEAD_DIM))
    angles = position[:, None] * frequency[None, :]
    cosine = jnp.cos(angles)[:, None, :]
    sine_vals = jnp.sin(angles)[:, None, :]
    score_scale = 1.0 / math.sqrt(HEAD_DIM)

    x_low = xor_order(tokens)
    g_low = xor_order(cotangent)
    inputs = x_low.astype(F32)
    scale_one = row_scales(inputs)
    normed_attn = (inputs * scale_one * gain_one).astype(BF)
    qkv = dot(normed_attn, w_qkv)
    heads_here = q_cols // HEAD_DIM
    kv_here = k_cols // HEAD_DIM
    group_size = heads_here // kv_here
    q_heads = qkv[:, :q_cols].reshape(row_count, heads_here, HEAD_DIM)
    k_heads = qkv[:, q_cols : q_cols + k_cols].reshape(row_count, kv_here, HEAD_DIM)
    v_bf = qkv[:, q_cols + k_cols :].astype(BF)
    q_scales, k_scales = row_scales(q_heads), row_scales(k_heads)
    q_bf = rotate_pairs(q_heads * q_scales * gain_q, cosine, sine_vals).astype(BF)
    k_bf = rotate_pairs(k_heads * k_scales * gain_k, cosine, sine_vals).astype(BF)
    kv_all = lax.all_gather(
        jnp.concatenate([k_bf.reshape(row_count, k_cols), v_bf], axis=1), "ctx", axis=0, tiled=True
    )
    k_all = kv_all[:, :k_cols].reshape(tree_total, kv_here, HEAD_DIM)
    v_all = kv_all[:, k_cols:].reshape(tree_total, kv_here, HEAD_DIM)
    q_grouped = q_bf.reshape(row_count, kv_here, group_size, HEAD_DIM)
    scores = (
        jnp.einsum("tkgd,skd->kgts", q_grouped, k_all, preferred_element_type=F32) * score_scale
    )
    scores = jnp.where(allowed[None, None], scores, -1e30)
    row_max = jnp.max(scores, axis=-1, keepdims=True)
    weights = jnp.exp(scores - row_max)
    prob_all = weights / jnp.sum(weights, axis=-1, keepdims=True)
    prob_bf = prob_all.astype(BF)
    mixture = jnp.einsum("kgts,skd->tkgd", prob_bf, v_all, preferred_element_type=F32)
    mixture_bf = mixture.reshape(row_count, heads_here * HEAD_DIM).astype(BF)
    own_inputs = inputs[:chunk]
    hidden = own_inputs + scatter_sum(outer_cols(mixture_bf, wo_t))

    scale_two = row_scales(hidden)
    normed_own = (hidden * scale_two * gain_two).astype(BF)
    normed_mlp = jnp.concatenate(gather_rows(normed_own), axis=0)
    gate_pre = dot(normed_mlp, wg_full)
    up_pre = dot(normed_mlp, wu_full)
    gate_sig = jax.nn.sigmoid(gate_pre)
    gate_act = gate_pre * gate_sig
    inner_bf = (gate_act * up_pre).astype(BF)

    grad_down_t = grad_scatter(g_low, inner_bf)
    grad_inner = dot(g_low, wd_t)
    grad_gate_pre = (grad_inner * up_pre * gate_sig * (1.0 + gate_pre * (1.0 - gate_sig))).astype(
        BF
    )
    grad_up_pre = (grad_inner * gate_act).astype(BF)
    grad_normed_mlp = scatter_sum(
        outer_cols(grad_gate_pre, wg_full) + outer_cols(grad_up_pre, wu_full)
    )
    grad_gate = grad_scatter(normed_mlp, grad_gate_pre)
    grad_up = grad_scatter(normed_mlp, grad_up_pre)
    own_cotangent = g_low[:chunk].astype(F32)
    grad_hidden_norm, gain_two_terms = norm_back(grad_normed_mlp, hidden, gain_two, scale_two)
    gain_two_part = jnp.sum(gain_two_terms, axis=0)
    grad_hidden = own_cotangent + grad_hidden_norm
    grad_attn_bf = jnp.concatenate(gather_rows(grad_hidden.astype(BF)), axis=0)

    result_own = (hidden + scatter_sum(outer_cols(inner_bf, wd_t))).astype(BF)
    result = xor_order(jnp.concatenate(gather_rows(result_own), axis=0))

    grad_out_t = grad_scatter(grad_attn_bf, mixture_bf)
    grad_mixture = (
        dot(grad_attn_bf, wo_t).astype(BF).reshape(row_count, kv_here, group_size, HEAD_DIM)
    )
    grad_probs = jnp.einsum("tkgd,skd->kgts", grad_mixture, v_all, preferred_element_type=F32)
    grad_v_all = jnp.einsum("kgts,tkgd->skd", prob_bf, grad_mixture, preferred_element_type=F32)
    row_total = jnp.sum(prob_all * grad_probs, axis=-1, keepdims=True)
    grad_scores = (prob_all * (grad_probs - row_total)).astype(BF)
    grad_q = (
        jnp.einsum("kgts,skd->tkgd", grad_scores, k_all, preferred_element_type=F32) * score_scale
    )
    grad_k_all = (
        jnp.einsum("kgts,tkgd->skd", grad_scores, q_grouped, preferred_element_type=F32)
        * score_scale
    )
    grad_kv = lax.psum_scatter(
        jnp.concatenate(
            [grad_k_all.reshape(tree_total, k_cols), grad_v_all.reshape(tree_total, k_cols)], axis=1
        ).astype(BF),
        "ctx",
        scatter_dimension=0,
        tiled=True,
    )
    grad_q = grad_q.reshape(row_count, heads_here, HEAD_DIM)
    grad_k = grad_kv[:, :k_cols].reshape(row_count, kv_here, HEAD_DIM).astype(F32)
    grad_v_bf = grad_kv[:, k_cols:]
    grad_q_heads, q_gain_terms = norm_back(
        rotate_back(grad_q, cosine, sine_vals), q_heads, gain_q, q_scales
    )
    grad_k_heads, k_gain_terms = norm_back(
        rotate_back(grad_k, cosine, sine_vals), k_heads, gain_k, k_scales
    )
    grad_qkv_raw = jnp.concatenate(
        [
            grad_q_heads.reshape(row_count, q_cols).astype(BF),
            grad_k_heads.reshape(row_count, k_cols).astype(BF),
            grad_v_bf,
        ],
        axis=1,
    )
    grad_qkv = grad_scatter(normed_attn, grad_qkv_raw)
    partial_back = outer_cols(grad_qkv_raw, w_qkv)
    gain_one_part = jnp.sum(partial_back * inputs * scale_one, axis=0)
    grad_normed_attn = scatter_sum(partial_back)
    grad_input_norm, unused_terms = norm_back(
        grad_normed_attn, own_inputs, gain_one, scale_one[:chunk]
    )
    grad_own = lax.optimization_barrier((grad_hidden + grad_input_norm).astype(BF))
    grad_tokens = xor_order(jnp.concatenate(gather_rows(grad_own), axis=0)).astype(F32)

    block = lax.axis_index("dp") * ctx_size + lax.axis_index("ctx")
    summed = lax.psum(
        jnp.concatenate(
            [
                gain_one_part,
                gain_two_part,
                jnp.sum(q_gain_terms, axis=(0, 1)),
                jnp.sum(k_gain_terms, axis=(0, 1)),
            ]
        ),
        ("dp", "ctx", "tensor"),
    )
    gain_grads, place = [], 0
    for size, part in zip(gain_sizes, gain_parts):
        gain_grads.append(lax.dynamic_slice_in_dim(summed, place + block * size, size))
        place += part.shape[0]

    return (
        result,
        grad_tokens,
        grad_qkv[:, :q_cols].astype(F32),
        grad_qkv[:, q_cols : q_cols + k_cols].astype(F32),
        grad_qkv[:, q_cols + k_cols :].astype(F32),
        grad_out_t.T.astype(F32),
        grad_gate.astype(F32),
        grad_up.astype(F32),
        grad_down_t.T.astype(F32),
        *gain_grads,
    )


def solution(mesh):
    rows = P(ROWS, None)
    cols = P(ROWS, "tensor")
    flipped = P("tensor", ROWS)
    vector = P(ROWS)
    return jax.shard_map(
        on_device,
        mesh=mesh,
        in_specs=(
            rows,
            P("dp", None),
            P("dp", None),
            cols,
            cols,
            cols,
            flipped,
            cols,
            cols,
            flipped,
            vector,
            vector,
            vector,
            vector,
            rows,
        ),
        out_specs=(
            rows,
            rows,
            cols,
            cols,
            cols,
            flipped,
            cols,
            cols,
            flipped,
            vector,
            vector,
            vector,
            vector,
        ),
        check_vma=False,
    )
```
